32 devices in a mesh: grp: 2 (over y), section: 2 (over x), lat: 2 (over core), lon: 4 (over z).
Axes of the slice: x: 2, y: 2, z: 4, core: 2. Of those that a mesh axis runs over, the one named last changes fastest.
Arguments:
- section_input: bfloat16 [2, 64, 32, 1536], P('section', ('grp', 'lat'), 'lon'), parts along dimension 1, may hold values from -6 to 6
- fresh_input: bfloat16 [64, 32, 1536], P(('grp', 'lat'), 'lon'), parts along dimension 0, may hold values from -6 to 6
- offsets: int32 [4], P('grp'), parts along dimension 0, may hold values from 1 to 4, as said below
- regions: int32 [64, 32], P(('grp', 'lat'), 'lon'), parts along dimension 0, may hold values from 0 to 8, as said below
- up_weight: bfloat16 [2, 1536, 3072], P('section', 'lon', 'lat'), may hold values from -0.15625 to 0.15625
- up_bias: float32 [2, 3072], P('section', 'lat'), may hold values from -3 to 3
- down_weight: bfloat16 [2, 3072, 1536], P('section', 'lat', 'lon'), may hold values from -0.109375 to 0.109375
- mlp_gain: float32 [2, 1536], P('section'), may hold values from 0.5 to 1.5
- qkv_weight: bfloat16 [2, 1536, 3, 768], P('section', 'lon', None, 'lat'), may hold values from -0.15625 to 0.15625
- logit_scale: float32 [2, 12], P('section', 'lat'), may hold values from 2 to 20
- position_bias: float32 [2, 12, 64, 64], P('section', 'lat'), may hold values from 0 to 8
- out_weight: bfloat16 [2, 768, 1536], P('section', 'lat', 'lon'), may hold values from -0.21875 to 0.21875
- attn_gain: float32 [2, 1536], P('section'), may hold values from 0.5 to 1.5
Outputs:
- handed: bfloat16 [2, 64, 32, 1536], P('section', ('grp', 'lat'), 'lon'), parts along dimension 1
- opened: bfloat16 [2, 64, 32, 1536], P('section', ('grp', 'lat'), 'lon'), parts along dimension 1
The draws below stay inside these ranges and needn't reach their ends.
There are 2 independent parts, one for each index of `grp`. The reference program is written for one: setup_inputs(seed, part) draws one part's arguments, and reference() takes and returns one part's arrays. A program takes and returns all parts, laid end to end along the dimension named above; an argument that names none is the same for every part. Nothing has to cross between parts.
Inputs may be any that keep to these rules, and one draw needn't show every extreme that they name: offsets[0] is the latitude shift and offsets[1] the longitude shift; at least one of them equals 4. `regions`: the shifted-window region id of each token of the rolled grid: 3 * a + b, where a is 0 for rows i < 24, 1 for 24 <= i < 32 - offsets[0] and 2 for the rest, and b is the same for columns with 32 and offsets[1].
All inputs are finite; a program needn't handle non-finite values.
Results may differ from the reference program's by a relative error of at most 0.014.
Values may be sent and summed in bfloat16 or wider, within the bound.
No kernel may reach another device: no remote copies, remote signals or barrier semaphores. Data moves between devices by JAX's collectives and lax.ppermute only.
A program may use at most 64 MiB of HBM per device.

```python
import math
import jax
import jax.numpy as jnp
from jax import lax

D = 1536
HIDDEN_SIZE = 3072
ATT_HEADS = 12
HEAD_DIM = 64
W = 8
SECTIONS = 2
NLAT = 32
NLON = 32
N_LAT = 2


def shift_pair(key):
    key_one, key_two = jax.random.split(jax.random.fold_in(key, 11))
    largest = W // 2
    first = jax.random.randint(key_one, (), 1, largest + 1)
    second = jax.random.randint(key_two, (), 1, largest + 1)
    second = jnp.where(first < largest, largest, second)
    return jnp.stack([first, second]).astype(jnp.int32)


def draw_offsets(key, part):
    return shift_pair(key)


def slab_ids(count, shift):
    place = jnp.arange(count, dtype=jnp.int32)
    middle = (place >= count - W).astype(jnp.int32)
    last = (place >= count - shift).astype(jnp.int32)
    return middle + last


def draw_regions(key, part):
    pair = shift_pair(key)
    lat_slab = slab_ids(NLAT, pair[0])
    lon_slab = slab_ids(NLON, pair[1])
    return (3 * lat_slab[:, None] + lon_slab[None, :]).astype(jnp.int32)


def shard_levels(own_key, extent, cuts, least, top_value):
    loudness = 1.0
    for axis_at, blocks in cuts:
        steps = jax.random.uniform(jax.random.fold_in(jax.random.fold_in(own_key, 6), axis_at), (blocks,), jnp.float32, least / len(cuts), top_value / len(cuts))
        loudness = loudness * jnp.repeat(jnp.exp(steps), extent[axis_at] // blocks).reshape((-1,) + (1,) * (len(extent) - 1 - axis_at))
    return loudness


def gaussian(own_key, dims, scale, most, cuts=(), held_as=jnp.bfloat16):
    array = scale * jax.random.normal(own_key, dims, jnp.float32)
    if cuts:
        array = array * shard_levels(own_key, dims, cuts, -0.22, 0.18)
    return jnp.clip(array, -most, most).astype(held_as)


def setup_inputs(seed: int = 0, part: int = 0) -> dict:
    seeds = jax.random.split(jax.random.key(seed), 14)
    part_splits = jax.random.split(jax.random.fold_in(seeds[13], part), 14)
    section_input = gaussian(part_splits[0], (SECTIONS, NLAT, NLON, D), 1.0, 6.0, ((0, 2), (1, 2), (2, 4)))
    fresh_input = gaussian(part_splits[1], (NLAT, NLON, D), 1.0, 6.0, ((0, 2), (1, 4)))
    offsets = draw_offsets(jax.random.fold_in(jax.random.fold_in(seeds[13], part), 71), part)
    regions = draw_regions(jax.random.fold_in(jax.random.fold_in(seeds[13], part), 71), part)
    up_weight = gaussian(seeds[4], (SECTIONS, D, HIDDEN_SIZE), D ** -0.5, 0.15625, ((0, 2), (1, 4), (2, 2)))
    up_bias = gaussian(seeds[5], (SECTIONS, HIDDEN_SIZE), 0.5, 3.0, ((0, 2), (1, 2)), jnp.float32)
    down_weight = gaussian(seeds[6], (SECTIONS, HIDDEN_SIZE, D), HIDDEN_SIZE ** -0.5, 0.109375, ((0, 2), (1, 2), (2, 4)))
    mlp_gain = jnp.clip(1.0 + 0.1 * jax.random.normal(seeds[7], (SECTIONS, D), jnp.float32), 0.5, 1.5)
    qkv_weight = gaussian(seeds[8], (SECTIONS, D, 3, ATT_HEADS * HEAD_DIM), D ** -0.5, 0.15625, ((0, 2), (1, 4), (3, 2)))
    logit_scale = jnp.clip(jnp.exp(math.log(20.0) - 2.3025851 * jax.random.uniform(seeds[9], (SECTIONS, ATT_HEADS), jnp.float32) ** shard_levels(seeds[9], (SECTIONS, ATT_HEADS), ((0, 2), (1, 2)), -0.2, 0.2)), 2.0, 20.0)
    position_bias = jnp.clip(8.0 * jax.random.uniform(seeds[10], (SECTIONS, ATT_HEADS, W * W, W * W), jnp.float32) ** shard_levels(seeds[10], (SECTIONS, ATT_HEADS, W * W, W * W), ((0, 2), (1, 2)), -0.2, 0.2), 0.0, 8.0)
    out_weight = gaussian(seeds[11], (SECTIONS, ATT_HEADS * HEAD_DIM, D), (ATT_HEADS * HEAD_DIM) ** -0.5, 0.21875, ((0, 2), (1, 2), (2, 4)))
    attn_gain = jnp.clip(1.0 + 0.1 * jax.random.normal(seeds[12], (SECTIONS, D), jnp.float32), 0.5, 1.5)
    return {"section_input": section_input, "fresh_input": fresh_input, "offsets": offsets, "regions": regions, "up_weight": up_weight, "up_bias": up_bias, "down_weight": down_weight, "mlp_gain": mlp_gain, "qkv_weight": qkv_weight, "logit_scale": logit_scale, "position_bias": position_bias, "out_weight": out_weight, "attn_gain": attn_gain}


def layer_norm(total, norm_gain):
    mean = lax.optimization_barrier(jnp.mean(total, axis=-1, keepdims=True))
    centered = total - mean
    variance = lax.optimization_barrier(jnp.mean(centered * centered, axis=-1, keepdims=True))
    return centered * lax.rsqrt(variance + 1e-05) * norm_gain

def windows(values, side):
    height, breadth = (values.shape[0], values.shape[1])
    rest = values.shape[2:]
    blocks = values.reshape((height // side, side, breadth // side, side) + rest)
    blocks = jnp.moveaxis(blocks, 2, 1)
    return blocks.reshape((-1, side * side) + rest)

def unwindow(values, height, breadth, side):
    rest = values.shape[2:]
    blocks = values.reshape((height // side, breadth // side, side, side) + rest)
    blocks = jnp.moveaxis(blocks, 1, 2)
    return blocks.reshape((height, breadth) + rest)

def attend(packed, region_marks, head_scale, pos_bias):
    blocks = windows(packed, W).astype(jnp.float32)
    query_rows = blocks[:, :, 0]
    key_rows = blocks[:, :, 1]
    value_rows = blocks[:, :, 2]
    inner_dot = jnp.einsum('wihd,wjhd->whij', query_rows, key_rows)
    query_norm = lax.rsqrt(lax.optimization_barrier(jnp.sum(query_rows * query_rows, axis=-1)) + 1e-06)
    key_norm = lax.rsqrt(lax.optimization_barrier(jnp.sum(key_rows * key_rows, axis=-1)) + 1e-06)
    cosine = inner_dot * jnp.transpose(query_norm, (0, 2, 1))[:, :, :, None]
    cosine = cosine * jnp.transpose(key_norm, (0, 2, 1))[:, :, None, :]
    score = cosine * head_scale[None, :, None, None] + pos_bias[None]
    marked = windows(region_marks, W)
    same_region = (marked[:, :, None] == marked[:, None, :])[:, None]
    raw_weights = jnp.where(same_region, jnp.exp(score), jnp.float32(0.0))
    weights = (raw_weights / lax.optimization_barrier(jnp.sum(raw_weights, axis=-1, keepdims=True))).astype(jnp.bfloat16)
    context = jnp.einsum('whij,wjhd->wihd', weights.astype(jnp.float32), value_rows)
    return context.astype(jnp.bfloat16)

def block_sum(left, right, parts):
    block = left.shape[1] // parts
    total = jnp.zeros((left.shape[0], right.shape[1]), jnp.float32)
    for index in range(parts):
        term = jnp.dot(left[:, index * block:(index + 1) * block], right[index * block:(index + 1) * block], preferred_element_type=jnp.float32)
        rounded = lax.optimization_barrier(term.astype(jnp.bfloat16))
        total = total + rounded.astype(jnp.float32)
    return total

def reference(section_input, fresh_input, offsets, regions, up_weight, up_bias, down_weight, mlp_gain, qkv_weight, logit_scale, position_bias, out_weight, attn_gain):
    shift_lat = offsets[0]
    shift_lon = offsets[1]
    handed_list = []
    opened_list = []
    entering = fresh_input
    for section in range(SECTIONS):
        flat_rows = section_input[section].reshape(-1, D)
        pre_act = jnp.dot(flat_rows, up_weight[section], preferred_element_type=jnp.float32) + up_bias[section]
        hidden = jax.nn.gelu(pre_act, approximate=False).astype(jnp.bfloat16)
        mlp_sum = block_sum(hidden, down_weight[section], N_LAT)
        handed = (flat_rows.astype(jnp.float32) + layer_norm(mlp_sum, mlp_gain[section])).astype(jnp.bfloat16)
        handed_list.append(handed.reshape(NLAT, NLON, D))
        rolled = jnp.roll(entering, (-shift_lat, -shift_lon), axis=(0, 1))
        packed = jnp.dot(rolled.reshape(-1, D), qkv_weight[section].reshape(D, -1), preferred_element_type=jnp.float32)
        packed = packed.astype(jnp.bfloat16).reshape(NLAT, NLON, 3, ATT_HEADS, HEAD_DIM)
        context = attend(packed, regions, logit_scale[section], position_bias[section])
        context = unwindow(context, NLAT, NLON, W).reshape(NLAT * NLON, ATT_HEADS * HEAD_DIM)
        attn_sum = block_sum(context, out_weight[section], N_LAT)
        branch = layer_norm(attn_sum, attn_gain[section]).astype(jnp.bfloat16).reshape(NLAT, NLON, D)
        branch = jnp.roll(branch, (shift_lat, shift_lon), axis=(0, 1))
        opened = (entering.astype(jnp.float32) + branch.astype(jnp.float32)).astype(jnp.bfloat16)
        opened_list.append(opened)
        entering = handed_list[-1]
    return (jnp.stack(handed_list), jnp.stack(opened_list))
```

```python
import jax
import jax.numpy as jnp
from jax import lax
from jax.sharding import PartitionSpec as P

W = 8


def layer_norm(total, norm_gain):
    mean = jnp.mean(total, axis=-1, keepdims=True)
    centered = total - mean
    variance = jnp.mean(centered * centered, axis=-1, keepdims=True)
    return centered * lax.rsqrt(variance + 1e-05) * norm_gain


def windows(values, side):
    height, breadth = (values.shape[0], values.shape[1])
    rest = values.shape[2:]
    blocks = values.reshape((height // side, side, breadth // side, side) + rest)
    blocks = jnp.moveaxis(blocks, 2, 1)
    return blocks.reshape((-1, side * side) + rest)


def unwindow(values, height, breadth, side):
    rest = values.shape[2:]
    blocks = values.reshape((height // side, breadth // side, side, side) + rest)
    blocks = jnp.moveaxis(blocks, 1, 2)
    return blocks.reshape((height, breadth) + rest)


def attend(packed, region_marks, head_scale, pos_bias):
    blocks = windows(packed, W)
    query_rows = blocks[:, :, 0]
    key_rows = blocks[:, :, 1]
    value_rows = blocks[:, :, 2]
    inner_dot = jnp.einsum(
        "wihd,wjhd->whij", query_rows, key_rows, preferred_element_type=jnp.float32
    )
    query_wide = query_rows.astype(jnp.float32)
    key_wide = key_rows.astype(jnp.float32)
    query_norm = lax.rsqrt(jnp.sum(query_wide * query_wide, axis=-1) + 1e-06)
    key_norm = lax.rsqrt(jnp.sum(key_wide * key_wide, axis=-1) + 1e-06)
    cosine = inner_dot * jnp.transpose(query_norm, (0, 2, 1))[:, :, :, None]
    cosine = cosine * jnp.transpose(key_norm, (0, 2, 1))[:, :, None, :]
    score = cosine * head_scale[None, :, None, None] + pos_bias[None]
    marked = windows(region_marks, W)
    same_region = (marked[:, :, None] == marked[:, None, :])[:, None]
    raw_weights = jnp.where(same_region, jnp.exp(score), jnp.float32(0.0))
    weights = (raw_weights / jnp.sum(raw_weights, axis=-1, keepdims=True)).astype(jnp.bfloat16)
    context = jnp.einsum("whij,wjhd->wihd", weights, value_rows, preferred_element_type=jnp.float32)
    return context.astype(jnp.bfloat16)


def xor_route(axis, bit):
    return [(i, i ^ bit) for i in range(lax.axis_size(axis))]


def swap(block, axis):
    return lax.ppermute(block, axis, xor_route(axis, 1))


def spread(own, other):
    count = lax.axis_size("lon")
    even = lax.axis_index("grp") == 0
    blocks = [own] + [None] * (count - 1)
    ready = jnp.where(even, own, other)
    for k in range(2, count, 2):
        route = [
            (g * count + i, g * count + (i ^ (k + g))) for g in range(2) for i in range(count)
        ]
        fetched = lax.ppermute(ready, ("grp", "lon"), route)
        handed = swap(fetched, "grp")
        blocks[k] = jnp.where(even, fetched, handed)
        blocks[k + 1] = jnp.where(even, handed, fetched)
    blocks[1] = lax.ppermute(other, "lon", xor_route("lon", 1))
    return blocks


def per_device(
    section_input,
    fresh_input,
    offsets,
    regions,
    up_weight,
    up_bias,
    down_weight,
    mlp_gain,
    qkv_weight,
    logit_scale,
    position_bias,
    out_weight,
    attn_gain,
):
    tile_in = section_input[0]
    height, breadth, width = tile_in.shape
    lon_count = lax.axis_size("lon")
    lon_at = lax.axis_index("lon")
    lat_at = lax.axis_index("lat")
    sections = lax.axis_size("section")
    odd = lon_at % 2
    depth = up_weight.shape[1]
    units = up_weight.shape[2] // 2
    flat = tile_in.reshape(-1, width)
    rows = flat.shape[0]

    pair_rows = lax.ppermute(flat, "lon", xor_route("lon", 1))
    mine = jnp.concatenate([flat, pair_rows], 0)
    tokens = jnp.concatenate([mine, swap(mine, "lat")], 0)

    direct = lax.axis_size("grp") == 2 and lon_count & (lon_count - 1) == 0 and depth % 128 == 0

    def gathered(block, join_axis, half_axis):
        if half_axis is None:
            own = other = block
        else:
            own = lax.dynamic_slice_in_dim(block, odd * units, units, half_axis)
            other = lax.dynamic_slice_in_dim(block, (1 - odd) * units, units, half_axis)
        if direct:
            return spread(own, other)
        whole = lax.all_gather(block, "lon", axis=join_axis, tiled=True)
        if half_axis is not None:
            whole = lax.dynamic_slice_in_dim(whole, odd * units, units, half_axis)
        return [whole]

    up_blocks = gathered(up_weight[0], 0, 1)
    down_blocks = gathered(down_weight[0], 1, 0)
    qkv_blocks = gathered(jnp.moveaxis(qkv_weight[0], 1, 0), 1, None)
    out_blocks = gathered(out_weight[0], 1, None)
    pieces = len(up_blocks)

    def begin(k):
        return (lon_at ^ k) * depth if direct else 0

    def columns(array, k):
        return lax.dynamic_slice_in_dim(array, begin(k), width // pieces, 1)

    pre_act = sum(
        jnp.dot(columns(tokens, k), up_blocks[k], preferred_element_type=jnp.float32)
        for k in range(pieces)
    )
    bias = lax.dynamic_slice_in_dim(up_bias[0], odd * units, units, 0)
    hidden = jax.nn.gelu(pre_act + bias, approximate=False).astype(jnp.bfloat16)

    sums = []
    for k in range(pieces):
        term = jnp.dot(hidden, down_blocks[k], preferred_element_type=jnp.float32)
        from_lat = swap(term[2 * rows :].astype(jnp.bfloat16), "lat")
        sums.append(term[: 2 * rows] + from_lat.astype(jnp.float32))
    mlp_sum = jnp.zeros((rows, width), jnp.float32)
    for k in range(pieces):
        mate = k ^ 1 if direct else k
        from_pair = lax.ppermute(
            sums[mate][rows:].astype(jnp.bfloat16), "lon", xor_route("lon", 1)
        )
        piece = sums[k][:rows] + from_pair.astype(jnp.float32)
        mlp_sum = lax.dynamic_update_slice_in_dim(mlp_sum, piece, begin(k), 1)
    handed_flat = flat.astype(jnp.float32) + layer_norm(mlp_sum, mlp_gain[0])
    handed = handed_flat.astype(jnp.bfloat16).reshape(height, breadth, width)

    strip_width = W // 2
    first_section = lax.axis_index("section") == 0
    fresh_strip = lax.ppermute(
        fresh_input[:, :strip_width],
        "lon",
        [((i + 1) % lon_count, i) for i in range(lon_count)],
    )
    passed = lax.ppermute(handed, "section", [(s, s + 1) for s in range(sections - 1)])
    passed_strip = lax.ppermute(
        handed[:, :strip_width],
        ("section", "lon"),
        [
            (s * lon_count + (i + 1) % lon_count, (s + 1) * lon_count + i)
            for s in range(sections - 1)
            for i in range(lon_count)
        ],
    )
    entering = jnp.where(first_section, fresh_input, passed)
    after_strip = jnp.where(first_section, fresh_strip, passed_strip)
    shift_lat = offsets[0]
    shift_lon = offsets[1]
    rolled = lax.dynamic_slice_in_dim(
        jnp.concatenate([entering, after_strip], 1), shift_lon, breadth, 1
    )
    grid = jnp.concatenate([rolled, swap(rolled, "lat")], 0)
    grid_height = 2 * height
    start = (shift_lat + height * lat_at) % grid_height
    grid = lax.dynamic_slice_in_dim(jnp.concatenate([grid, grid], 0), start, grid_height, 0)
    marks = jnp.concatenate([regions, swap(regions, "lat")], 0)
    grid_marks = jnp.where(lat_at == 0, marks, jnp.roll(marks, height, 0))
    flat_grid = grid.reshape(-1, width)
    heads_local = logit_scale.shape[1]
    head_size = qkv_weight.shape[3] // heads_local
    packed = jnp.concatenate(
        [
            sum(
                jnp.dot(columns(flat_grid, k), qkv_blocks[k][j], preferred_element_type=jnp.float32)
                for k in range(pieces)
            ).astype(jnp.bfloat16)[:, None]
            for j in range(3)
        ],
        1,
    ).reshape(grid_height, breadth, 3, heads_local, head_size)
    context = attend(packed, grid_marks, logit_scale[0], position_bias[0])
    context = unwindow(context, grid_height, breadth, W).reshape(
        grid_height * breadth, heads_local * head_size
    )
    out_terms = jnp.zeros((grid_height * breadth, width), jnp.float32)
    for k in range(pieces):
        term = jnp.dot(context, out_blocks[k], preferred_element_type=jnp.float32)
        out_terms = lax.dynamic_update_slice_in_dim(out_terms, term, begin(k), 1)
    back = (grid_height - start) % grid_height
    out_terms = out_terms.reshape(grid_height, breadth, width)
    out_terms = lax.dynamic_slice_in_dim(
        jnp.concatenate([out_terms, out_terms], 0), back, grid_height, 0
    )
    from_lat = swap(out_terms[height:].astype(jnp.bfloat16), "lat")
    attn_sum = out_terms[:height] + from_lat.astype(jnp.float32)
    branch = layer_norm(attn_sum, attn_gain[0]).astype(jnp.bfloat16)
    tail_strip = lax.ppermute(
        branch[:, -strip_width:], "lon", [((i - 1) % lon_count, i) for i in range(lon_count)]
    )
    branch = lax.dynamic_slice_in_dim(
        jnp.concatenate([tail_strip, branch], 1), strip_width - shift_lon, breadth, 1
    )
    opened = (entering.astype(jnp.float32) + branch.astype(jnp.float32)).astype(jnp.bfloat16)
    return (handed[None], opened[None])


def solution(mesh):
    return jax.shard_map(
        per_device,
        mesh=mesh,
        in_specs=(
            P("section", ("grp", "lat"), "lon", None),
            P(("grp", "lat"), "lon", None),
            P("grp"),
            P(("grp", "lat"), "lon"),
            P("section", "lon", "lat"),
            P("section", "lat"),
            P("section", "lat", "lon"),
            P("section", None),
            P("section", "lon", None, "lat"),
            P("section", "lat"),
            P("section", "lat", None, None),
            P("section", "lat", "lon"),
            P("section", None),
        ),
        out_specs=(
            P("section", ("grp", "lat"), "lon", None),
            P("section", ("grp", "lat"), "lon", None),
        ),
        check_vma=False,
    )
```
